32 devices in a mesh: gx: 8 (over y, x, core), gy: 4 (over z).
Axes of the slice: x: 2, y: 2, z: 4, core: 2. Of those that a mesh axis runs over, the one named last changes fastest.
Arguments:
- resid: bfloat16 [128, 16384], P(('gx', 'gy')), may hold values from -6 to 6
- query: bfloat16 [128, 16384], P(('gx', 'gy')), may hold values from -6 to 6
- key_new: bfloat16 [128, 1024], P(('gx', 'gy')), may hold values from -6 to 6
- value_new: bfloat16 [128, 1024], P(('gx', 'gy')), may hold values from -6 to 6
- cache_keys: bfloat16 [128, 128, 1024], P(('gx', 'gy'))
- cache_values: bfloat16 [128, 128, 1024], P(('gx', 'gy')), may hold values from -6 to 6
- lengths: int32 [128], P(('gx', 'gy')), may hold values from 1 to 128, as said below
- norm_gain: bfloat16 [16384], replicated, may hold values from 0.5 to 1.5
- gate_weight: bfloat16 [16384, 26624], P('gx', 'gy'), may hold values from -0.046875 to 0.046875
- up_weight: bfloat16 [16384, 26624], P('gx', 'gy'), may hold values from -0.046875 to 0.046875
- down_weight: bfloat16 [26624, 16384], P('gy', 'gx'), may hold values from -0.0390625 to 0.0390625
Outputs:
- layer_out: bfloat16 [128, 16384], P(('gx', 'gy'))
The draws below stay inside these ranges and needn't reach their ends.
Inputs may be any that keep to these rules, and one draw needn't show every extreme that they name: `lengths`: some row has all 128 positions live.
All inputs are finite; a program needn't handle non-finite values.
Results may differ from the reference program's by a relative error of at most 0.0057.
Values may be sent and summed in bfloat16 or wider, within the bound.
A program may use at most 192 MiB of HBM per device.

```python
import jax
import jax.numpy as jnp
from jax import lax

D = 16384
FF = 26624
HQ = 128
KV = 8
HD = 128
CACHE = 128
ROWS = 128


def draw_cache_keys(key, part):
    base = jnp.clip(jax.random.normal(key, (ROWS, CACHE, KV * HD), jnp.float32), -4.0, 4.0)
    return base.astype(jnp.bfloat16)


def draw_lengths(key, part):
    drawn = jax.random.randint(key, (ROWS,), 1, CACHE + 1, jnp.int32)
    picked = jax.random.randint(jax.random.fold_in(key, 7), (), 0, ROWS, jnp.int32)
    places = jnp.arange(ROWS, dtype=jnp.int32)
    return jnp.where(places == picked, jnp.int32(CACHE), drawn)


def block_scale(own_key, shape, pieces, smallest, high):
    level, own = 1.0, jax.random.fold_in(own_key, 6)
    for position, parts in pieces:
        draws = jnp.exp(jax.random.uniform(jax.random.fold_in(own, position), (parts,), jnp.float32, smallest / len(pieces), high / len(pieces)))
        level = level * jnp.repeat(draws, shape[position] // parts).reshape([-1 if axis == position else 1 for axis in range(len(shape))])
    return level


def scatter_about(stream_key, shape, deviation, bound, split=(), kind=jnp.bfloat16):
    result = jax.random.normal(stream_key, shape, jnp.float32) * deviation
    if len(split) > 0:
        result = block_scale(stream_key, shape, split, -0.22, 0.18) * result
    return jnp.clip(result, min=-bound, max=bound).astype(kind)


def setup_inputs(seed: int = 0) -> dict:
    splits = jax.random.split(jax.random.key(seed), 12)
    return {
        "resid": scatter_about(splits[0], (ROWS, D), 1.0, 6.0, ((0, 32),)),
        "query": scatter_about(splits[1], (ROWS, D), 1.0, 6.0, ((0, 32),)),
        "key_new": scatter_about(splits[2], (ROWS, KV * HD), 1.0, 6.0, ((0, 32),)),
        "value_new": scatter_about(splits[3], (ROWS, KV * HD), 1.0, 6.0, ((0, 32),)),
        "cache_keys": draw_cache_keys(jax.random.fold_in(splits[11], 71), 0),
        "cache_values": scatter_about(splits[5], (ROWS, CACHE, KV * HD), 1.0, 6.0, ((0, 32),)),
        "lengths": draw_lengths(jax.random.fold_in(splits[11], 71), 0),
        "norm_gain": jnp.clip(1.0 + 0.1 * jax.random.normal(splits[7], (D,), jnp.float32), 0.5, 1.5).astype(jnp.bfloat16),
        "gate_weight": scatter_about(splits[8], (D, FF), D ** -0.5, 0.046875, ((0, 8), (1, 4))),
        "up_weight": scatter_about(splits[9], (D, FF), D ** -0.5, 0.046875, ((0, 8), (1, 4))),
        "down_weight": scatter_about(splits[10], (FF, D), FF ** -0.5, 0.0390625, ((0, 4), (1, 8))),
    }


def attend_row(query, key_new, value_new, cache_keys, cache_values, length):
    scale_factor = HD ** (-0.5)
    heads = query.astype(jnp.float32).reshape(KV, HQ // KV, HD)
    keys = cache_keys.astype(jnp.float32).reshape(CACHE, KV, HD)
    values = cache_values.astype(jnp.float32).reshape(CACHE, KV, HD)
    knew = key_new.astype(jnp.float32).reshape(KV, HD)
    vnew = value_new.astype(jnp.float32).reshape(KV, HD)
    scores = jnp.einsum('kgd,pkd->kgp', heads, keys) * scale_factor
    places = jnp.arange(CACHE, dtype=jnp.int32)
    scores = jnp.where(places[None, None, :] < length, scores, jnp.float32(-1e+30))
    own = jnp.einsum('kgd,kd->kg', heads, knew) * scale_factor
    top = jnp.maximum(lax.optimization_barrier(jnp.max(scores, axis=-1)), own)
    expo = jnp.exp(scores - top[..., None])
    own_expo = jnp.exp(own - top)
    total = lax.optimization_barrier(jnp.sum(expo, axis=-1)) + own_expo
    probs = (expo / total[..., None]).astype(jnp.bfloat16).astype(jnp.float32)
    own_prob = (own_expo / total).astype(jnp.bfloat16).astype(jnp.float32)
    mixed = jnp.einsum('kgp,pkd->kgd', probs, values) + own_prob[..., None] * vnew[:, None, :]
    return mixed.reshape(HQ * HD)

def reference(resid, query, key_new, value_new, cache_keys, cache_values, lengths, norm_gain, gate_weight, up_weight, down_weight):
    attended = lax.map(lambda a: attend_row(*a), (query, key_new, value_new, cache_keys, cache_values, lengths))
    mid = (resid.astype(jnp.float32) + attended).astype(jnp.bfloat16)
    midf = mid.astype(jnp.float32)
    inverse = lax.rsqrt(lax.optimization_barrier(jnp.mean(midf * midf, axis=-1, keepdims=True)) + 1e-05)
    normed = (midf * inverse * norm_gain.astype(jnp.float32)).astype(jnp.bfloat16)
    gate = jnp.dot(normed, gate_weight, preferred_element_type=jnp.float32)
    up = jnp.dot(normed, up_weight, preferred_element_type=jnp.float32)
    act = (jax.nn.silu(gate) * up).astype(jnp.bfloat16)
    ffn = jnp.dot(act, down_weight, preferred_element_type=jnp.float32)
    return (midf + ffn).astype(jnp.bfloat16)
```

```python
import functools

import jax
import jax.numpy as jnp
from jax import lax
from jax.experimental import pallas as pl
from jax.experimental.pallas import tpu as pltpu
from jax.sharding import PartitionSpec as P

KV = 8
HD = 128
MESH = pl.DeviceIdType.MESH
F32 = jnp.float32
BF16 = jnp.bfloat16


def kernel(
    cfg,
    lengths,
    resid,
    query,
    key_new,
    value_new,
    gain,
    cache_keys,
    cache_values,
    gate_hbm,
    up_hbm,
    down_hbm,
    out,
    kbuf,
    vbuf,
    mid,
    nbuf,
    xbuf,
    xs,
    gbuf,
    ubuf,
    dbuf,
    sums,
    recvs,
    agbuf,
    acc,
    obuf,
    rbuf,
    cache_sem,
    gate_sem,
    up_sem,
    down_sem,
    x_send,
    x_recv,
    o_send,
    o_recv,
    rs_send,
    rs_recv,
    ag_send,
    ag_recv,
):
    X, Y, K, C, NC, SG, SD = cfg
    n = X * Y
    gi, gj = lax.axis_index("gx"), lax.axis_index("gy")
    me = gi * Y + gj
    rloc, D = resid.shape
    span = cache_keys.shape[1]
    Dk = D // X
    N = xs.shape[0]
    G = D // (KV * HD)
    bits = [(gi // 2**s) % 2 for s in range(K)]
    partner = [gi + (1 - 2 * bits[s]) * 2**s for s in range(K)]

    barrier = pltpu.get_barrier_semaphore()

    @pl.loop(1, n)
    def _(d):
        t = (me + d) % n
        pl.semaphore_signal(barrier, inc=1, device_id=(t // Y, t % Y), device_id_type=MESH)

    kcopy = pltpu.make_async_copy(cache_keys, kbuf, cache_sem.at[0])
    vcopy = pltpu.make_async_copy(cache_values, vbuf, cache_sem.at[1])
    kcopy.start()
    vcopy.start()

    def gate_copy(c):
        cols = pl.ds(pl.multiple_of(c * C, C), C)
        return pltpu.make_async_copy(gate_hbm.at[:, cols], gbuf.at[c % SG], gate_sem.at[c % SG])

    def up_copy(c):
        cols = pl.ds(pl.multiple_of(c * C, C), C)
        return pltpu.make_async_copy(up_hbm.at[:, cols], ubuf.at[c % SG], up_sem.at[c % SG])

    def down_copy(c):
        rows = pl.ds(pl.multiple_of(c * C, C), C)
        return pltpu.make_async_copy(down_hbm.at[rows, :], dbuf.at[c % SD], down_sem.at[c % SD])

    @pl.loop(0, SG)
    def _(c):
        gate_copy(c).start()
        up_copy(c).start()

    @pl.loop(0, SD)
    def _(c):
        down_copy(c).start()

    M, S = G * rloc, rloc * span
    col = lax.broadcasted_iota(jnp.int32, (M, S), 1)
    row = lax.broadcasted_iota(jnp.int32, (M, S), 0) % rloc
    limit = jnp.zeros((M, S), jnp.int32)
    for r in range(rloc):
        limit = jnp.where(row == r, r * span + lengths[r], limit)
    live = (col >= row * span) & (col < limit)
    kcopy.wait()
    vcopy.wait()
    scale = HD ** (-0.5)

    def head(k, square):
        wide = pl.ds(pl.multiple_of(k * G * HD, G * HD), G * HD)
        one = pl.ds(pl.multiple_of(k * HD, HD), HD)
        q = query[:, wide].astype(F32)
        q = jnp.concatenate([q[:, g * HD : (g + 1) * HD] for g in range(G)], axis=0)
        kn = jnp.concatenate([key_new[:, one].astype(F32)] * G, axis=0)
        vn = jnp.concatenate([value_new[:, one].astype(F32)] * G, axis=0)
        keys = kbuf[:, :, one].reshape(S, HD)
        values = vbuf[:, :, one].reshape(S, HD)
        s = lax.dot_general(
            q.astype(BF16), keys, (((1,), (1,)), ((), ())), preferred_element_type=F32
        )
        s = jnp.where(live, s * scale, -1e30)
        own = jnp.sum(q * kn, axis=1, keepdims=True) * scale
        top = jnp.maximum(jnp.max(s, axis=1, keepdims=True), own)
        e = jnp.where(live, jnp.exp(s - top), 0.0)
        eo = jnp.exp(own - top)
        total = jnp.sum(e, axis=1, keepdims=True) + eo
        p = (e / total).astype(BF16)
        po = (eo / total).astype(BF16).astype(F32)
        mixed = jnp.dot(p, values, preferred_element_type=F32) + po * vn
        att = jnp.concatenate([mixed[g * rloc : (g + 1) * rloc] for g in range(G)], axis=1)
        m = (resid[:, wide].astype(F32) + att).astype(BF16)
        mid[:, wide] = m
        mf = m.astype(F32)
        return square + jnp.sum(mf * mf, axis=1, keepdims=True)

    square = lax.fori_loop(0, KV, head, jnp.zeros((rloc, 1), F32))
    inverse = lax.rsqrt(square / D + 1e-05)

    @pl.loop(0, X)
    def _(i):
        part = pl.ds(pl.multiple_of(i * Dk, Dk), Dk)
        nbuf[i] = (mid[:, part].astype(F32) * inverse * gain[:, part].astype(F32)).astype(BF16)

    xbuf[me] = nbuf[gi]
    pl.semaphore_wait(barrier, n - 1)

    @pl.loop(1, n)
    def _(d):
        t = (me + d) % n
        pltpu.make_async_remote_copy(
            src_ref=nbuf.at[t // Y],
            dst_ref=xbuf.at[me],
            send_sem=x_send,
            recv_sem=x_recv,
            device_id=(t // Y, t % Y),
            device_id_type=MESH,
        ).start()

    acc[...] = jnp.zeros_like(acc)
    pltpu.make_async_copy(xbuf.at[pl.ds(0, n - 1)], xbuf.at[pl.ds(0, n - 1)], x_recv).wait()
    per = 16 // rloc

    @pl.loop(0, N // 16)
    def _(b):
        rows = [xbuf[b * per + a].astype(F32) for a in range(per)]
        xs[pl.ds(pl.multiple_of(b * 16, 16), 16), :] = jnp.concatenate(rows, axis=0).astype(BF16)

    ALL = slice(None)

    def rs_copy(s, c):
        return pltpu.make_async_remote_copy(
            src_ref=sums[s].at[(c,) + (ALL,) * (K - s - 1) + (1 - bits[s],)],
            dst_ref=recvs[s].at[c],
            send_sem=rs_send.at[s],
            recv_sem=rs_recv.at[s, c],
            device_id=(partner[s], gj),
            device_id_type=MESH,
        )

    order = list(range(1, K)) + [0]

    def ag_copy(a, c, incoming=False):
        done = order[:a]
        idx = (c,)
        for b in range(K - 1, -1, -1):
            if b in done:
                idx += (ALL,)
            elif b == order[a] and incoming:
                idx += (1 - bits[b],)
            else:
                idx += (bits[b],)
        return pltpu.make_async_remote_copy(
            src_ref=agbuf.at[idx],
            dst_ref=agbuf.at[idx],
            send_sem=ag_send.at[a],
            recv_sem=ag_recv.at[a, c],
            device_id=(partner[order[a]], gj),
            device_id_type=MESH,
        )

    def stage_matmul(c):
        gate_copy(c).wait()
        x = xs[...]
        shape = (2,) * K + (N // X, C)
        g = jnp.dot(x, gbuf[c % SG], preferred_element_type=F32)
        sums[0][(c,) + (ALL,) * (K + 1) + (pl.ds(0, C),)] = g.astype(BF16).reshape(shape)
        up_copy(c).wait()
        u = jnp.dot(x, ubuf[c % SG], preferred_element_type=F32)
        sums[0][(c,) + (ALL,) * (K + 1) + (pl.ds(C, C),)] = u.astype(BF16).reshape(shape)
        rs_copy(0, c).start()

        @pl.when(c + SG < NC)
        def _():
            gate_copy(c + SG).start()
            up_copy(c + SG).start()

    def stage_reduce(s, c):
        rs_copy(s - 1, c).wait_recv()
        kept = sums[s - 1][(c,) + (ALL,) * (K - s) + (bits[s - 1],)].astype(F32)
        v = kept + recvs[s - 1][c].astype(F32)
        if s < K:
            sums[s][c] = v.astype(BF16)
            rs_copy(s, c).start()
        else:
            gate, up = v[:, :C], v[:, C:]
            act = gate / (1.0 + jnp.exp(-gate)) * up
            agbuf[(c,) + tuple(bits[b] for b in range(K - 1, -1, -1))] = act.astype(BF16)
            ag_copy(0, c).start()

    def stage_gather(a, c):
        ag_copy(a - 1, c, True).wait_recv()
        ag_copy(a, c).start()

    NW = min(512, Dk)

    def stage_down(c):
        ag_copy(K - 1, c, True).wait_recv()
        down_copy(c).wait()
        act = agbuf[c].reshape(N, C)
        for w in range(Dk // NW):
            cols = pl.ds(w * NW, NW)
            acc[:, cols] += jnp.dot(act, dbuf[c % SD, :, cols], preferred_element_type=F32)

        @pl.when(c + SD < NC)
        def _():
            down_copy(c + SD).start()

    stages = [stage_matmul]
    stages += [functools.partial(stage_reduce, s) for s in range(1, K + 1)]
    stages += [functools.partial(stage_gather, a) for a in range(1, K)]
    stages += [stage_down]

    @pl.loop(0, NC + len(stages) - 1)
    def _(t):
        for s, stage in enumerate(stages):
            c = t - s

            @pl.when((c >= 0) & (c < NC))
            def _():
                stage(c)

    @pl.loop(0, N // 8)
    def _(b):
        v = acc[pl.ds(pl.multiple_of(b * 8, 8), 8), :].astype(BF16)
        for a in range(8 // rloc):
            obuf[b * (8 // rloc) + a] = v[a * rloc : (a + 1) * rloc]

    @pl.loop(1, n)
    def _(d):
        t = (me + d) % n
        pltpu.make_async_remote_copy(
            src_ref=obuf.at[t],
            dst_ref=rbuf.at[me],
            send_sem=o_send,
            recv_sem=o_recv,
            device_id=(t // Y, t % Y),
            device_id_type=MESH,
        ).start()

    rbuf[me] = obuf[me]
    pltpu.make_async_copy(rbuf.at[pl.ds(0, n - 1)], rbuf.at[pl.ds(0, n - 1)], o_recv).wait()

    @pl.loop(0, X)
    def _(i):
        part = pl.ds(pl.multiple_of(i * Dk, Dk), Dk)
        v = rbuf[i * Y].astype(F32)
        for j in range(1, Y):
            v += rbuf[i * Y + j].astype(F32)
        out[:, part] = (mid[:, part].astype(F32) + v).astype(BF16)

    pltpu.make_async_copy(xbuf.at[pl.ds(0, n - 1)], xbuf.at[pl.ds(0, n - 1)], x_send).wait()
    pltpu.make_async_copy(rbuf.at[pl.ds(0, n - 1)], rbuf.at[pl.ds(0, n - 1)], o_send).wait()
    for s in range(K):
        pltpu.make_async_copy(recvs[s], recvs[s], rs_send.at[s]).wait()
    for a in range(K):
        idx = (ALL,)
        for b in range(K - 1, -1, -1):
            idx += (ALL,) if b in order[:a] else (bits[b],)
        pltpu.make_async_copy(agbuf.at[idx], agbuf.at[idx], ag_send.at[a]).wait()


def pick_chunk(width):
    c = 512
    while width % c:
        c //= 2
    return c


def on_device(
    X,
    Y,
    resid,
    query,
    key_new,
    value_new,
    cache_keys,
    cache_values,
    lengths,
    norm_gain,
    gate_weight,
    up_weight,
    down_weight,
):
    rloc, D = resid.shape
    n = X * Y
    N = rloc * n
    K = X.bit_length() - 1
    Dk, F = gate_weight.shape
    C = pick_chunk(F)
    NC = F // C
    SG, SD = min(7, NC), min(6, NC)
    R = N // X
    sums = [pltpu.VMEM((NC,) + (2,) * (K - s) + (R, 2 * C), BF16) for s in range(K)]
    recvs = [pltpu.VMEM((NC,) + (2,) * (K - s - 1) + (R, 2 * C), BF16) for s in range(K)]
    DMA = pltpu.SemaphoreType.DMA
    vmem = pl.BlockSpec(memory_space=pltpu.VMEM)
    hbm = pl.BlockSpec(memory_space=pl.ANY)
    scratch = [
        pltpu.VMEM(cache_keys.shape, BF16),
        pltpu.VMEM(cache_values.shape, BF16),
        pltpu.VMEM((rloc, D), BF16),
        pltpu.VMEM((X, rloc, Dk), BF16),
        pltpu.VMEM((n, rloc, Dk), BF16),
        pltpu.VMEM((N, Dk), BF16),
        pltpu.VMEM((SG, Dk, C), BF16),
        pltpu.VMEM((SG, Dk, C), BF16),
        pltpu.VMEM((SD, C, Dk), BF16),
        sums,
        recvs,
        pltpu.VMEM((NC,) + (2,) * K + (R, C), BF16),
        pltpu.VMEM((N, Dk), F32),
        pltpu.VMEM((n, rloc, Dk), BF16),
        pltpu.VMEM((n, rloc, Dk), BF16),
        DMA((2,)),
        DMA((SG,)),
        DMA((SG,)),
        DMA((SD,)),
        DMA,
        DMA,
        DMA,
        DMA,
        DMA((K,)),
        DMA((K, NC)),
        DMA((K,)),
        DMA((K, NC)),
    ]
    return pl.pallas_call(
        functools.partial(kernel, (X, Y, K, C, NC, SG, SD)),
        out_shape=jax.ShapeDtypeStruct((rloc, D), BF16),
        in_specs=[pl.BlockSpec(memory_space=pltpu.SMEM)] + [vmem] * 5 + [hbm] * 5,
        out_specs=vmem,
        scratch_shapes=scratch,
        compiler_params=pltpu.CompilerParams(
            collective_id=0, has_side_effects=True, vmem_limit_bytes=62 << 20
        ),
        name="layer",
    )(
        lengths,
        resid,
        query,
        key_new,
        value_new,
        norm_gain.reshape(1, D),
        cache_keys,
        cache_values,
        gate_weight,
        up_weight,
        down_weight,
    )


def solution(mesh):
    rows = P(("gx", "gy"), None)
    placed = (rows,) * 4 + (P(("gx", "gy"), None, None),) * 2
    placed += (P(("gx", "gy")), P(), P("gx", "gy"), P("gx", "gy"), P("gy", "gx"))
    return jax.shard_map(
        functools.partial(on_device, mesh.shape["gx"], mesh.shape["gy"]),
        mesh=mesh,
        in_specs=placed,
        out_specs=rows,
        check_vma=False,
    )
```
